256 devices in a mesh: rep: 32 (over x, z), tp: 8 (over y, core).
Axes of the slice: x: 4, y: 4, z: 8, core: 2. Of those that a mesh axis runs over, the one named last changes fastest.
Arguments:
- hidden_in: bfloat16 [1024, 3584], P('rep'), may hold values from -6 to 6
- k_cache: bfloat16 [1024, 8, 64, 128], P('rep', 'tp'), may hold values from -300 to 300, as said below
- v_cache: bfloat16 [1024, 8, 64, 128], P('rep', 'tp'), may hold values from -6 to 6
- lengths: int32 [1024], replicated, may hold values from 1 to 127, 65536 in all
- routes: int32 [1024, 1], replicated, may hold values from 0 to 31; in each aligned block of 32 rows (0 to 31, 32 to 63, ...) at most 2 rows name the same one
- w_query: bfloat16 [3584, 2048], P(None, 'tp'), may hold values from -0.09375 to 0.09375
- b_query: bfloat16 [2048], P('tp'), may hold values from -3 to 3
- w_key: bfloat16 [3584, 512], P(None, 'tp'), may hold values from -0.09375 to 0.09375
- b_key: bfloat16 [512], P('tp'), may hold values from -3 to 3
- w_value: bfloat16 [3584, 512], P(None, 'tp'), may hold values from -0.09375 to 0.09375
- b_value: bfloat16 [512], P('tp'), may hold values from -3 to 3
- w_out: bfloat16 [2048, 3584], P('tp'), may hold values from -0.125 to 0.125
- gain_in: bfloat16 [3584], replicated, may hold values from 0.25 to 1.75
- gain_out: bfloat16 [3584], replicated, may hold values from 0.25 to 1.75
- w_head: bfloat16 [152064, 3584], P(('rep', 'tp')), may hold values from -0.09375 to 0.09375
Outputs:
- final_norm: float32 [2048], P(('rep', 'tp'))
- top_logit: float32 [2048], P(('rep', 'tp'))
- k_cache_out: bfloat16 [2048, 8, 64, 128], P('rep', 'tp')
- v_cache_out: bfloat16 [2048, 8, 64, 128], P('rep', 'tp')
The draws below stay inside these ranges and needn't reach their ends.
Inputs may be any that keep to these rules, and one draw needn't show every extreme that they name: `routes`: within the 32 requests of one replica at most 2 name the same replica, and in every draw some replica is named exactly 2 times by some replica's requests. `k_cache`: keys are already rotated to their positions.
All inputs are finite; a program needn't handle non-finite values.
Results may differ from the reference program's by a relative error of at most 0.0022.
Values may be sent and summed in bfloat16 or wider, within the bound.
No kernel may reach another device: no remote copies, remote signals or barrier semaphores. Data moves between devices by JAX's collectives and lax.ppermute only.
A program may use at most 128 MiB of HBM per device.

```python
import math
import jax
import jax.numpy as jnp
import numpy as np
from jax import lax

D = 3584
HD = 128
V_DEV = 594
SLOTS = 32
MAXLEN = 128
HEADS = 16
KVH = 4
HALF = 64
CAP = 2
SERVE = 64
REQS = 1024
VOCAB = 152064
N_REP = 32
N_TP = 8
DEVICES = 256


def draw_k_cache(key, part):
    base = jnp.clip(jax.random.normal(key, (REQS, N_TP, HALF, HD), jnp.float32), -6.0, 6.0)
    return base.astype(jnp.bfloat16)


def block_scale(own_key, shape, cuts, low, top_value):
    gain, own = 1.0, jax.random.fold_in(own_key, 6)
    for axis_at, shards_of in cuts:
        draws = jnp.exp(jax.random.uniform(jax.random.fold_in(own, axis_at), (shards_of,), jnp.float32, low / len(cuts), top_value / len(cuts)))
        gain = gain * jnp.repeat(draws, shape[axis_at] // shards_of).reshape([-1 if axis == axis_at else 1 for axis in range(len(shape))])
    return gain


def profile(number_of, total, most, slope):
    weights = [(1 << 20) // math.isqrt(grade ** slope) + 1 for grade in range(2, number_of + 1)]
    spare, counts = total - most - (number_of - 1), [1] * (number_of - 1)
    while spare > 0:
        candidates = [i for i in range(number_of - 1) if counts[i] < most]
        whole, remaining = sum([weights[i] for i in candidates]), spare
        for i in candidates:
            more = min(most - counts[i], max(1, remaining * weights[i] // whole), spare)
            counts[i] = counts[i] + more
            spare = spare - more
    return np.array([most] + counts)


def uneven_parts(stream_key, amount, total, reach, slope):
    if amount == 2:
        one = jax.random.randint(stream_key, (), max(1, total - reach), min(reach, total - 1) + 1)
        return jnp.stack([one, total - one])
    tallies = jnp.asarray(profile(amount, total, reach, slope), jnp.int32)
    couples = (amount - 1) // 2
    source_of, sink = tallies[1:1 + 2 * couples:2], tallies[2:2 + 2 * couples:2]
    slack = jnp.minimum(source_of - 1, reach - sink)
    moved = jax.random.randint(jax.random.fold_in(stream_key, 1), (couples,), 0, 1 << 20) % (slack + 1)
    tallies = tallies.at[1:1 + 2 * couples:2].set(source_of - moved).at[2:2 + 2 * couples:2].set(sink + moved)
    return tallies[jax.random.permutation(jax.random.fold_in(stream_key, 2), amount)]


def assign_block(stream_key, own, number, rows, number_of, top, most, slope):
    sequence = jax.random.permutation(stream_key, number_of)
    packed, ordinary = shares(number_of, rows * top, most, slope, True), shares(number_of, rows * top, most, slope, False)
    places = jnp.arange(number_of)

    def named(sizes, offset_by):
        used = int((sizes > 0).sum())
        fixed = max(1, used // 4)
        passed = fixed + (places - fixed + offset_by * (used - fixed)) % max(1, number_of - fixed)
        return jnp.zeros((number_of,), jnp.int32).at[sequence[jnp.where(places < fixed, places, passed)]].set(jnp.asarray(sizes, jnp.int32))

    sizes = jnp.where(number % 4 == 0, named(packed, number // 4), named(ordinary, number - number // 4 - 1))
    mixed = jax.random.permutation(jax.random.fold_in(own, 3), number_of)
    source_of, taker = mixed[0:number_of // 2 * 2:2], mixed[1:number_of // 2 * 2:2]
    slack = jnp.minimum(sizes[source_of] - 1, most - sizes[taker]) // 2
    slack = jnp.where((source_of == sequence[0]) | (taker == sequence[0]) | (sizes[taker] == 0), 0, jnp.maximum(slack, 0))
    passed = jax.random.randint(jax.random.fold_in(own, 4), (number_of // 2,), 0, 1 << 20) % (slack + 1)
    sizes = sizes.at[source_of].add(-passed).at[taker].add(passed)
    members = jnp.searchsorted(jnp.cumsum(sizes), jnp.arange(rows * top), side="right").astype(jnp.int32)
    grid = members.reshape(top, rows).T
    grid = grid[jax.random.permutation(jax.random.fold_in(own, 1), rows)]
    offset_by = jax.random.randint(jax.random.fold_in(own, 2), (rows, 1), 0, top)
    return jnp.take_along_axis(grid, (jnp.arange(top)[None, :] + offset_by) % top, axis=1)


def shares(count, total, limit, slope, full):
    weights = [(1 << 20) // math.isqrt(rank ** slope) + 1 for rank in range(1, count + 1)]
    largest = limit if full else min(limit, max(-(-total // count), total * weights[0] // sum(weights)))
    least = 1 if total - largest >= count - 1 else 0
    counts, rest = [largest] + [least] * (count - 1), total - largest - least * (count - 1)
    while rest > 0:
        movable = [i for i in range(1, count) if counts[i] < largest] or [i for i in range(1, count) if counts[i] < limit]
        whole, left = sum([weights[i] for i in movable]), rest
        for i in movable:
            more = min(limit - counts[i], max(1, left * weights[i] // whole), rest)
            counts[i] = counts[i] + more
            rest = rest - more
    return np.array(counts)


def bell_draw(stream_key, extent, width, reach, pieces=(), kind=jnp.bfloat16):
    drawn = width * jax.random.normal(stream_key, extent, jnp.float32)
    if pieces:
        drawn = drawn * block_scale(stream_key, extent, pieces, -0.22, 0.18)
    return jnp.clip(drawn, -reach, reach).astype(kind)


def setup_inputs(seed: int = 0) -> dict:
    seeds = jax.random.split(jax.random.key(seed), 16)
    hidden_in = bell_draw(seeds[0], (REQS, D), 1.0, 6.0, ((0, 32),))
    k_cache = draw_k_cache(jax.random.fold_in(seeds[15], 71), 0)
    v_cache = bell_draw(seeds[2], (REQS, N_TP, HALF, HD), 1.0, 6.0, ((0, 32), (1, 8)))
    lengths = uneven_parts(seeds[3], REQS, REQS * MAXLEN // 2, MAXLEN - 1, 2).astype(jnp.int32)
    routes_keys = jax.random.split(jax.random.fold_in(seeds[4], 1), REQS // SLOTS)
    routes_turns = jax.random.permutation(jax.random.fold_in(seeds[4], 3), REQS // SLOTS)
    routes = jax.vmap(lambda own, number: assign_block(jax.random.fold_in(seeds[4], 2), own, number, SLOTS, N_REP, 1, CAP, 2))(routes_keys, routes_turns).reshape((REQS, 1))
    w_query = bell_draw(seeds[5], (D, HEADS * HD), D ** -0.5, 0.09375, ((1, 8),))
    b_query = bell_draw(seeds[6], (HEADS * HD,), 0.5, 3.0, ((0, 8),))
    w_key = bell_draw(seeds[7], (D, KVH * HD), D ** -0.5, 0.09375, ((1, 8),))
    b_key = bell_draw(seeds[8], (KVH * HD,), 0.5, 3.0, ((0, 8),))
    w_value = bell_draw(seeds[9], (D, KVH * HD), D ** -0.5, 0.09375, ((1, 8),))
    b_value = bell_draw(seeds[10], (KVH * HD,), 0.5, 3.0, ((0, 8),))
    w_out = bell_draw(seeds[11], (HEADS * HD, D), (HEADS * HD) ** -0.5, 0.125, ((0, 8),))
    gain_in = jnp.clip(1.0 + 0.15 * jax.random.normal(seeds[12], (D,), jnp.float32), 0.25, 1.75).astype(jnp.bfloat16)
    gain_out = jnp.clip(1.0 + 0.15 * jax.random.normal(seeds[13], (D,), jnp.float32), 0.25, 1.75).astype(jnp.bfloat16)
    w_head = bell_draw(seeds[14], (VOCAB, D), D ** -0.5, 0.09375, ((0, 256),))
    return {"hidden_in": hidden_in, "k_cache": k_cache, "v_cache": v_cache, "lengths": lengths, "routes": routes, "w_query": w_query, "b_query": b_query, "w_key": w_key, "b_key": b_key, "w_value": w_value, "b_value": b_value, "w_out": w_out, "gain_in": gain_in, "gain_out": gain_out, "w_head": w_head}


def rotate(vals, positions):
    half = vals.shape[-1] // 2
    freq = 1000000.0 ** (-(jnp.arange(half, dtype=jnp.float32) * 2.0 / vals.shape[-1]))
    angle = positions[..., None] * freq
    first = vals[..., :half]
    second = vals[..., half:]
    return jnp.concatenate([first * jnp.cos(angle) - second * jnp.sin(angle), second * jnp.cos(angle) + first * jnp.sin(angle)], axis=-1)

def destinations(routes):
    flat = routes[:, 0].reshape(N_REP, SLOTS)
    onehot = (flat[:, :, None] == jnp.arange(N_REP, dtype=jnp.int32)[None, None, :]).astype(jnp.int32)
    rank = lax.optimization_barrier(jnp.sum((jnp.cumsum(onehot, axis=1) - onehot) * onehot, axis=2))
    source = jnp.arange(N_REP, dtype=jnp.int32)[:, None]
    return (flat * SERVE + source * CAP + rank).reshape(-1).astype(jnp.int32)

def one_request(args):
    queries, keys, values, key_new, value_new, length = args
    scale = 1.0 / HD ** 0.5
    scores = jnp.einsum('kgd,kpd->kgp', queries.astype(jnp.float32), keys.astype(jnp.float32), precision=lax.Precision.HIGHEST) * scale
    live = (jnp.arange(MAXLEN, dtype=jnp.int32) < length)[None, None, :]
    scores = jnp.where(live, scores, -1e+30)
    own = jnp.einsum('kgd,kd->kg', queries.astype(jnp.float32), key_new.astype(jnp.float32), precision=lax.Precision.HIGHEST) * scale
    peak = jnp.maximum(lax.optimization_barrier(jnp.max(scores, axis=2)), own)
    weights = jnp.where(live, jnp.exp(scores - peak[..., None]), 0.0)
    own_weight = jnp.exp(own - peak)
    total = lax.optimization_barrier(jnp.sum(weights, axis=2)) + own_weight
    mixed = jnp.einsum('kgp,kpd->kgd', weights, values.astype(jnp.float32), precision=lax.Precision.HIGHEST)
    mixed = mixed + own_weight[..., None] * value_new.astype(jnp.float32)[:, None, :]
    return (mixed / total[..., None]).reshape(-1).astype(jnp.bfloat16)

def reference(hidden_in, k_cache, v_cache, lengths, routes, w_query, b_query, w_key, b_key, w_value, b_value, w_out, gain_in, gain_out, w_head):
    eps = 1e-06
    xf = hidden_in.astype(jnp.float32)
    normed_in = (xf * lax.rsqrt(lax.optimization_barrier(jnp.mean(xf * xf, axis=1, keepdims=True)) + eps) * gain_in.astype(jnp.float32)).astype(jnp.bfloat16)
    positions = lengths.astype(jnp.float32)[:, None]
    query = (jnp.dot(normed_in, w_query, preferred_element_type=jnp.float32) + b_query.astype(jnp.float32)).reshape(REQS, HEADS, HD)
    query = rotate(query, positions).astype(jnp.bfloat16)
    key_raw = (jnp.dot(normed_in, w_key, preferred_element_type=jnp.float32) + b_key.astype(jnp.float32)).astype(jnp.bfloat16).reshape(REQS, KVH, HD)
    key_new = rotate(key_raw.astype(jnp.float32), positions).astype(jnp.bfloat16)
    value_new = (jnp.dot(normed_in, w_value, preferred_element_type=jnp.float32) + b_value.astype(jnp.float32)).astype(jnp.bfloat16).reshape(REQS, KVH, HD)
    keys = k_cache.reshape(REQS, KVH, MAXLEN, HD)
    values = v_cache.reshape(REQS, KVH, MAXLEN, HD)
    grouped = query.reshape(REQS, KVH, HEADS // KVH, HD)
    attn = lax.map(one_request, (grouped, keys, values, key_new, value_new, lengths))
    state = (xf + jnp.dot(attn, w_out, preferred_element_type=jnp.float32)).astype(jnp.bfloat16)
    sf = state.astype(jnp.float32)
    ms = lax.optimization_barrier(jnp.mean(sf * sf, axis=1))
    rms = jnp.sqrt(ms)
    normed = (sf * lax.rsqrt(ms + eps)[:, None] * gain_out.astype(jnp.float32)).astype(jnp.bfloat16)
    blocks = w_head.reshape(DEVICES, V_DEV, D)

    def step(best, block):
        logits = lax.dot_general(normed, block, (((1,), (1,)), ((), ())), preferred_element_type=jnp.float32)
        return (jnp.maximum(best, lax.optimization_barrier(jnp.max(logits, axis=1))), None)
    best, _ = lax.scan(step, jnp.full((REQS,), -jnp.inf, jnp.float32), blocks)
    dest = destinations(routes)
    written = (jnp.arange(MAXLEN, dtype=jnp.int32)[None, :] == lengths[:, None])[:, None, :, None]
    keys_full = jnp.where(written, key_new[:, :, None, :], keys).reshape(REQS, N_TP, HALF, HD)
    values_full = jnp.where(written, value_new[:, :, None, :], values).reshape(REQS, N_TP, HALF, HD)
    k_cache_out = jnp.zeros((N_REP * SERVE, N_TP, HALF, HD), jnp.bfloat16).at[dest].set(keys_full)
    v_cache_out = jnp.zeros((N_REP * SERVE, N_TP, HALF, HD), jnp.bfloat16).at[dest].set(values_full)
    final_norm = jnp.zeros((N_REP * SERVE,), jnp.float32).at[dest].set(rms)
    top_logit = jnp.zeros((N_REP * SERVE,), jnp.float32).at[dest].set(best)
    return (final_norm, top_logit, k_cache_out, v_cache_out)
```

```python
import jax
import jax.numpy as jnp
from jax import lax
from jax.sharding import Mesh, PartitionSpec as P

REP = ("x", "z")
TP = ("y", "c")
ALL = ("x", "z", "y", "c")


def shifted(value, axis, distance):
    size = lax.axis_size(axis)
    return lax.ppermute(value, axis, [((i + distance) % size, i) for i in range(size)])


def spread(value, axis):
    size = lax.axis_size(axis)
    copies = jnp.broadcast_to(value[None], (size,) + value.shape)
    return lax.all_to_all(copies, axis, split_axis=0, concat_axis=0, tiled=True)


def rotate(vals, cos, sin):
    half = vals.shape[-1] // 2
    first = vals[..., :half]
    second = vals[..., half:]
    return jnp.concatenate([first * cos - second * sin, second * cos + first * sin], axis=-1)


def per_device(
    hidden_in,
    k_cache,
    v_cache,
    lengths,
    routes,
    w_query,
    b_query,
    w_key,
    b_key,
    w_value,
    b_value,
    w_out,
    gain_in,
    gain_out,
    w_head,
):
    f32 = jnp.float32
    bf16 = jnp.bfloat16
    eps = 1e-06
    n_z = lax.axis_size("z")
    n_y = lax.axis_size("y")
    n_rep = lax.axis_size("x") * n_z
    n_tp = n_y * 2
    y_pos = lax.axis_index("y")
    c_pos = lax.axis_index("c")
    rep_pos = lax.axis_index("x") * n_z + lax.axis_index("z")
    even = c_pos == 0
    slots, width = hidden_in.shape
    half_len, head_size = k_cache.shape[2:]
    cap = 2
    serve = n_rep * cap
    cols = width // n_y
    rows = slots // 2

    scaled = (w_head.astype(f32) * gain_out.astype(f32)[None, :]).astype(bf16)
    head = jnp.concatenate([scaled, shifted(scaled, "c", 1)], axis=0)
    head_parts = [
        lax.dynamic_slice_in_dim(head, ((y_pos + d) % n_y) * cols, cols, 1) for d in range(n_y)
    ]

    flat = routes[:, 0].reshape(n_rep, slots)
    earlier = (flat[:, None, :] == flat[:, :, None]) & (
        jnp.arange(slots)[None, None, :] < jnp.arange(slots)[None, :, None]
    )
    rank = jnp.sum(earlier.astype(jnp.int32), axis=2)
    bucket = flat * cap + rank
    own_bucket = lax.dynamic_slice_in_dim(bucket, rep_pos, 1, 0)[0]
    lens = lax.dynamic_slice_in_dim(lengths, rep_pos * slots, slots, 0)

    xf = hidden_in.astype(f32)
    normed_in = (
        xf * lax.rsqrt(jnp.mean(xf * xf, axis=1, keepdims=True) + eps) * gain_in.astype(f32)
    ).astype(bf16)
    half = head_size // 2
    freq = 1000000.0 ** (-(jnp.arange(half, dtype=f32) * 2.0 / head_size))
    angle = lens.astype(f32)[:, None] * freq
    cos, sin = jnp.cos(angle), jnp.sin(angle)
    query = (
        jnp.dot(normed_in, w_query, preferred_element_type=f32) + b_query.astype(f32)
    ).reshape(slots, -1, head_size)
    query = rotate(query, cos[:, None], sin[:, None]).astype(bf16)
    key_part = (jnp.dot(normed_in, w_key, preferred_element_type=f32) + b_key.astype(f32)).astype(
        bf16
    )
    value_part = (
        jnp.dot(normed_in, w_value, preferred_element_type=f32) + b_value.astype(f32)
    ).astype(bf16)
    packed = jnp.concatenate([query.reshape(slots, -1), key_part, value_part], axis=1)
    other = shifted(packed, "c", 1)
    first = jnp.where(even, packed, other)
    second = jnp.where(even, other, packed)
    q_width = query.shape[1] * head_size
    k_width = key_part.shape[1]
    queries = jnp.concatenate([first[:, :q_width], second[:, :q_width]], axis=1).reshape(
        slots, -1, head_size
    )
    key_raw = jnp.concatenate(
        [first[:, q_width : q_width + k_width], second[:, q_width : q_width + k_width]], axis=1
    )
    value_new = jnp.concatenate(
        [first[:, q_width + k_width :], second[:, q_width + k_width :]], axis=1
    )
    key_new = rotate(key_raw.astype(f32), cos, sin).astype(bf16)

    keys = k_cache[:, 0]
    values = v_cache[:, 0]
    scale = 1.0 / head_size**0.5
    scores = jnp.einsum("sgd,spd->sgp", queries, keys, preferred_element_type=f32) * scale
    place = c_pos * half_len + jnp.arange(half_len, dtype=jnp.int32)
    live = (place[None, :] < lens[:, None])[:, None, :]
    scores = jnp.where(live, scores, -1e30)
    own_score = (
        jnp.sum(queries.astype(f32) * key_new.astype(f32)[:, None, :], axis=2) * scale
    )
    own_score = jnp.where(even, own_score, -1e30)
    peak = jnp.maximum(jnp.max(scores, axis=2), own_score)
    weights = jnp.where(live, jnp.exp(scores - peak[..., None]), 0.0)
    own_weight = jnp.where(even, jnp.exp(own_score - peak), 0.0)
    total = jnp.sum(weights, axis=2) + own_weight
    mixed = jnp.einsum("sgp,spd->sgd", weights.astype(bf16), values, preferred_element_type=f32)
    mixed = mixed + own_weight[..., None] * value_new.astype(f32)[:, None, :]
    state_all = jnp.concatenate(
        [
            mixed,
            jnp.broadcast_to(peak[..., None], peak.shape + (head_size,)),
            jnp.broadcast_to(total[..., None], total.shape + (head_size,)),
        ],
        axis=2,
    )
    keep = jnp.where(even, state_all[:, :2], state_all[:, 2:])
    give = jnp.where(even, state_all[:, 2:], state_all[:, :2])
    got = shifted(give, "c", 1)
    peak_keep = keep[..., head_size : head_size + 1]
    peak_got = got[..., head_size : head_size + 1]
    upper = jnp.maximum(peak_keep, peak_got)
    mine = jnp.exp(peak_keep - upper)
    theirs = jnp.exp(peak_got - upper)
    merged = (keep[..., :head_size] * mine + got[..., :head_size] * theirs) / (
        keep[..., 2 * head_size : 2 * head_size + 1] * mine
        + got[..., 2 * head_size : 2 * head_size + 1] * theirs
    )
    attn = merged.reshape(slots, -1).astype(bf16)

    partial = jnp.dot(attn, w_out, preferred_element_type=f32).astype(bf16)
    partial = partial.reshape(2, rows, n_y, cols).transpose(2, 0, 1, 3).reshape(n_tp, rows, cols)
    shares = lax.all_to_all(partial, TP, split_axis=0, concat_axis=0, tiled=True)
    own_x = lax.dynamic_slice(hidden_in, (c_pos * rows, y_pos * cols), (rows, cols))
    state = (own_x.astype(f32) + jnp.sum(shares.astype(f32), axis=0)).astype(bf16)

    gathered = spread(state, "z").reshape(n_z * rows, cols)
    gathered = spread(gathered, "x").reshape(n_rep * rows, cols)
    chunks = [gathered] + [shifted(gathered, "y", d) for d in range(1, n_y)]
    logits = 0.0
    squares = 0.0
    for chunk, weight in zip(chunks, head_parts):
        logits = logits + lax.dot_general(
            chunk, weight, (((1,), (1,)), ((), ())), preferred_element_type=f32
        )
        wide = chunk.astype(f32)
        squares = squares + jnp.sum(wide * wide, axis=1)
    ms = squares / width
    best = (jnp.max(logits, axis=1) * lax.rsqrt(ms + eps)).reshape(n_rep, 1, rows)
    rms = jnp.sqrt(ms).reshape(n_rep, 1, rows)

    own_rows = lax.dynamic_slice(bucket, (0, c_pos * rows), (n_rep, rows))
    hit = own_rows[:, None, :] == jnp.arange(serve, dtype=jnp.int32)[None, :, None]
    send_best = jnp.max(jnp.where(hit, best, -jnp.inf), axis=2)
    send_rms = jnp.max(jnp.where(hit, rms, -1.0), axis=2)
    send = jnp.stack([send_best, send_rms], axis=0).reshape(2, n_rep, n_rep, cap)
    send = send.transpose(2, 1, 0, 3).reshape(n_rep, n_tp, n_rep // n_tp, 2, cap)
    send = send.reshape(n_rep * n_tp, -1)
    arrived = jnp.max(lax.all_to_all(send, ALL, split_axis=0, concat_axis=0, tiled=True), axis=0)
    arrived = arrived.reshape(n_rep // n_tp, 2, cap)
    arrived_best = arrived[:, 0].reshape(-1)
    arrived_rms = arrived[:, 1].reshape(-1)
    taken = arrived_rms >= 0.0
    final_norm = jnp.where(taken, arrived_rms, 0.0)
    top_logit = jnp.where(taken, arrived_best, 0.0)

    written = (place[None, :] == lens[:, None])[:, :, None]
    keys_full = jnp.where(written, key_new[:, None, :], keys)
    values_full = jnp.where(written, value_new[:, None, :], values)
    hits = own_bucket[None, :] == jnp.arange(serve, dtype=jnp.int32)[:, None]
    pick = jnp.sum(jnp.where(hits, jnp.arange(slots, dtype=jnp.int32)[None, :], 0), axis=1)
    filled = jnp.any(hits, axis=1)[:, None, None]
    send_k = jnp.where(filled, keys_full[pick], jnp.zeros((), bf16))
    send_v = jnp.where(filled, values_full[pick], jnp.zeros((), bf16))
    got_k = lax.all_to_all(send_k, REP, split_axis=0, concat_axis=0, tiled=True)
    got_v = lax.all_to_all(send_v, REP, split_axis=0, concat_axis=0, tiled=True)
    return (final_norm, top_logit, got_k[:, None], got_v[:, None])


def solution(mesh):
    n_rep, n_tp = mesh.devices.shape
    fine = Mesh(mesh.devices.reshape(4, n_rep // 4, n_tp // 2, 2), ("x", "z", "y", "c"))
    in_specs = (
        P(REP, None),
        P(REP, TP, None, None),
        P(REP, TP, None, None),
        P(),
        P(),
        P(None, TP),
        P(TP),
        P(None, TP),
        P(TP),
        P(None, TP),
        P(TP),
        P(TP, None),
        P(),
        P(),
        P(ALL, None),
    )
    out_specs = (P(ALL), P(ALL), P(REP, TP, None, None), P(REP, TP, None, None))
    return jax.shard_map(
        per_device, mesh=fine, in_specs=in_specs, out_specs=out_specs, check_vma=False
    )
```

```python
import jax
import jax.numpy as jnp
from jax import lax
from jax.experimental import pallas as pl
from jax.experimental.pallas import tpu as pltpu
from jax.sharding import Mesh, PartitionSpec as P

REP = ("x", "z")
TP = ("y", "c")
ALL = ("x", "z", "y", "c")
HBM = pltpu.MemorySpace.HBM


def shifted(value, axis, distance):
    size = lax.axis_size(axis)
    return lax.ppermute(value, axis, [((i + distance) % size, i) for i in range(size)])


def spread(value, axis):
    size = lax.axis_size(axis)
    copies = jnp.broadcast_to(value[None], (size,) + value.shape)
    return lax.all_to_all(copies, axis, split_axis=0, concat_axis=0, tiled=True)


def rotate(vals, cos, sin):
    half = vals.shape[-1] // 2
    first = vals[..., :half]
    second = vals[..., half:]
    return jnp.concatenate([first * cos - second * sin, second * cos + first * sin], axis=-1)


def ring(block, axis):
    size = lax.axis_size(axis)

    def from_side(value, step):
        pairs = [
            (((i + (step if c == 0 else -step)) % size) * 2 + c, i * 2 + c)
            for i in range(size)
            for c in range(2)
        ]
        return lax.ppermute(value, (axis, "c"), pairs)

    first = from_side(block, 1)
    second = from_side(block, -1)
    return [block, first, from_side(first, 1), second]


def head_kernel(y_ref, *refs):
    sources = refs[:8]
    gain, row, lane, own, other, out, x, weights = refs[8:16]
    landed = refs[16:24]
    chunk_sems, weight_sems = refs[24:]
    f32 = jnp.float32
    bf16 = jnp.bfloat16
    copies = [
        pltpu.make_async_copy(source, target, chunk_sems.at[i])
        for i, (source, target) in enumerate(zip(sources, landed))
    ]
    vocab, width = own.shape
    split = vocab // 16 * 8
    tiles = [(i, low, high) for i in range(2) for low, high in ((0, split), (split, vocab))]
    loads = [
        pltpu.make_async_copy(
            (own, other)[i].at[low:high], weights.at[i, low:high], weight_sems.at[at]
        )
        for at, (i, low, high) in enumerate(tiles)
    ]
    for copy in copies:
        copy.start()
    n, quarter, cols = landed[0].shape
    sums = [0.0] * (2 * n)
    for copy in copies:
        copy.wait()
    for load in loads:
        load.start()
    for d in range(n):
        start_a = pl.multiple_of(y_ref[1, d] * cols, 128)
        start_b = pl.multiple_of(y_ref[0, d] * cols, 128)
        scale_a = gain[:, pl.ds(start_a, cols)].astype(f32)
        scale_b = gain[:, pl.ds(start_b, cols)].astype(f32)
        for i in range(2 * n):
            if i < n:
                piece, start, scale = landed[d][i], start_a, scale_a
            else:
                piece, start, scale = landed[i][d], start_b, scale_b
            wide = piece.astype(f32)
            sums[i] = sums[i] + jnp.sum(wide * wide, axis=1, keepdims=True)
            x[pl.ds(i * quarter, quarter), pl.ds(start, cols)] = (wide * scale).astype(bf16)
    dims = (((1,), (1,)), ((), ()))
    top = None
    for load, (i, low, high) in zip(loads, tiles):
        load.wait()
        logits = lax.dot_general(weights[i, low:high, :], x[...], dims, preferred_element_type=f32)
        peak = jnp.max(logits, axis=0, keepdims=True)
        top = peak if top is None else jnp.maximum(top, peak)

    ms = jnp.concatenate(sums, axis=0) / width
    here = lax.broadcasted_iota(jnp.int32, (out.shape[0], row.shape[1]), 0) == row[...]
    lanes = lax.broadcasted_iota(jnp.int32, (row.shape[1], out.shape[1]), 1)
    at = lane[...]
    place = (lanes == at).astype(f32)
    rest = jnp.where(lanes == at + 8, ms, 0.0) + (lanes == at + 16).astype(f32)
    exact = lax.Precision.HIGHEST
    out[...] = jnp.dot(
        jnp.where(here, top, 0.0), place, precision=exact, preferred_element_type=f32
    ) + jnp.dot(here.astype(f32), rest, precision=exact, preferred_element_type=f32)


def head(y_pos, chunks_a, chunks_b, gain, row, lane, own, other, targets):
    chunks = chunks_a + chunks_b
    vocab, width = own.shape
    count = row.shape[1]
    vmem = pl.BlockSpec(memory_space=pltpu.VMEM)
    hbm = pl.BlockSpec(memory_space=HBM)
    return pl.pallas_call(
        head_kernel,
        in_specs=[pl.BlockSpec(memory_space=pltpu.SMEM)]
        + [hbm] * len(chunks)
        + [vmem] * 3
        + [hbm] * 2,
        out_specs=vmem,
        scratch_shapes=[
            pltpu.VMEM((count, width), jnp.bfloat16),
            pltpu.VMEM((2, vocab, width), jnp.bfloat16),
        ]
        + [pltpu.VMEM(value.shape, value.dtype) for value in chunks]
        + [pltpu.SemaphoreType.DMA((len(chunks),)), pltpu.SemaphoreType.DMA((4,))],
        out_shape=jax.ShapeDtypeStruct((targets, 128), jnp.float32),
        compiler_params=pltpu.CompilerParams(vmem_limit_bytes=60 * 1024 * 1024),
        name="head",
    )(y_pos, *chunks, gain[None], row, lane, own, other)


def after_kernel(value, other, out):
    del other, out


def after(value, *others):
    hbm = pl.BlockSpec(memory_space=HBM)
    for other in others:
        value = pl.pallas_call(
            after_kernel,
            in_specs=[hbm, hbm],
            out_specs=hbm,
            out_shape=jax.ShapeDtypeStruct(value.shape, value.dtype),
            input_output_aliases={0: 0},
            name="after",
        )(value, other)
    return value


def project_kernel(x_ref, gain, bias, cos, sin, wq_ref, wk_ref, wv_ref, out, wq, wk, wv, sems):
    f32 = jnp.float32
    bf16 = jnp.bfloat16
    loads = [
        pltpu.make_async_copy(source, target, sems.at[i])
        for i, (source, target) in enumerate(((wq_ref, wq), (wk_ref, wk), (wv_ref, wv)))
    ]
    for load in loads:
        load.start()
    x = x_ref[...].astype(f32)
    mean = jnp.mean(x * x, axis=1, keepdims=True)
    normed = (x * lax.rsqrt(mean + 1e-06) * gain[...].astype(f32)).astype(bf16)
    for load in loads:
        load.wait()
    query = jnp.dot(normed, wq[...], preferred_element_type=f32)
    dims = (((1,), (1,)), ((), ()))
    rest = [
        lax.dot_general(normed, weight[...], dims, preferred_element_type=f32)
        for weight in (wk, wv)
    ]
    c, s = cos[...], sin[...]
    half = c.shape[1]
    at = query.shape[1]
    query = query + bias[:, :at].astype(f32)
    for low in range(0, at, 2 * half):
        first = query[:, low : low + half]
        second = query[:, low + half : low + 2 * half]
        out[:, low : low + 2 * half] = jnp.concatenate(
            [first * c - second * s, second * c + first * s], axis=1
        ).astype(bf16)
    out[:, at:] = (jnp.concatenate(rest, axis=1) + bias[:, at:].astype(f32)).astype(bf16)


def project(x, gain, wq, bq, wk, bk, wv, bv, cos, sin):
    width = wq.shape[1] + wk.shape[1] + wv.shape[1]
    vmem = pl.BlockSpec(memory_space=pltpu.VMEM)
    hbm = pl.BlockSpec(memory_space=HBM)
    weights = (wq, wk.T, wv.T)
    return pl.pallas_call(
        project_kernel,
        in_specs=[vmem] * 5 + [hbm] * 3,
        out_specs=vmem,
        out_shape=jax.ShapeDtypeStruct((x.shape[0], width), jnp.bfloat16),
        scratch_shapes=[pltpu.VMEM(w.shape, w.dtype) for w in weights]
        + [pltpu.SemaphoreType.DMA((3,))],
        compiler_params=pltpu.CompilerParams(vmem_limit_bytes=60 * 1024 * 1024),
        name="project",
    )(x, gain[None], jnp.concatenate([bq, bk, bv])[None], cos, sin, *weights)


def pack_kernel(pick, at, keys, values, key_new, value_new, out):
    half = keys.shape[2]
    place = lax.broadcasted_iota(jnp.int32, (half, keys.shape[3]), 0)

    def body(slot, carry):
        source = pick[slot]
        from_row = jnp.maximum(source, 0)
        live = jnp.broadcast_to(source, place.shape) >= 0
        written = place == at[from_row]
        for i, (cache, new) in enumerate(((keys, key_new), (values, value_new))):
            old = cache[from_row, 0].astype(jnp.float32)
            full = jnp.where(written, new[pl.ds(from_row, 1), :], old)
            out[slot, i * half : (i + 1) * half, :] = jnp.where(live, full, 0.0).astype(out.dtype)
        return carry

    lax.fori_loop(0, out.shape[0], body, 0, unroll=4)


def pack(pick, at, keys, values, key_new, value_new):
    _, _, half, head_size = keys.shape
    smem = pl.BlockSpec(memory_space=pltpu.SMEM)
    vmem = pl.BlockSpec(memory_space=pltpu.VMEM)
    return pl.pallas_call(
        pack_kernel,
        in_specs=[smem] * 2 + [vmem] * 4,
        out_specs=vmem,
        out_shape=jax.ShapeDtypeStruct((pick.shape[0], 2 * half, head_size), keys.dtype),
        compiler_params=pltpu.CompilerParams(vmem_limit_bytes=60 * 1024 * 1024),
        name="pack",
    )(pick, at, keys, values, key_new, value_new)


def settle_kernel(got, keys, values):
    half = keys.shape[2]
    keys[:, 0] = got[:, :half]
    values[:, 0] = got[:, half:]


def settle(got):
    serve, length, head_size = got.shape
    step = serve // 8
    shape = jax.ShapeDtypeStruct((serve, 1, length // 2, head_size), got.dtype)
    return pl.pallas_call(
        settle_kernel,
        grid=(8,),
        in_specs=[pl.BlockSpec((step, length, head_size), lambda i: (i, 0, 0))],
        out_specs=[pl.BlockSpec((step, 1, length // 2, head_size), lambda i: (i, 0, 0, 0))] * 2,
        out_shape=[shape, shape],
        name="settle",
    )(got)


def per_device(
    hidden_in,
    k_cache,
    v_cache,
    lengths,
    routes,
    w_query,
    b_query,
    w_key,
    b_key,
    w_value,
    b_value,
    w_out,
    gain_in,
    gain_out,
    w_head,
):
    f32 = jnp.float32
    bf16 = jnp.bfloat16
    eps = 1e-06
    n_z = lax.axis_size("z")
    n_y = lax.axis_size("y")
    n_rep = lax.axis_size("x") * n_z
    n_tp = n_y * 2
    y_pos = lax.axis_index("y")
    c_pos = lax.axis_index("c")
    rep_pos = lax.axis_index("x") * n_z + lax.axis_index("z")
    even = c_pos == 0
    slots, width = hidden_in.shape
    half_len, head_size = k_cache.shape[2:]
    cap = 2
    serve = n_rep * cap
    cols = width // n_y
    rows = slots // 2

    head_other = shifted(w_head, "c", 1)

    flat = routes[:, 0].reshape(n_rep, slots)
    earlier = (flat[:, None, :] == flat[:, :, None]) & (
        jnp.arange(slots)[None, None, :] < jnp.arange(slots)[None, :, None]
    )
    rank = jnp.sum(earlier.astype(jnp.int32), axis=2)
    bucket = flat * cap + rank
    own_bucket = lax.dynamic_slice_in_dim(bucket, rep_pos, 1, 0)[0]
    lens = lax.dynamic_slice_in_dim(lengths, rep_pos * slots, slots, 0)

    half = head_size // 2
    freq = 1000000.0 ** (-(jnp.arange(half, dtype=f32) * 2.0 / head_size))
    angle = lens.astype(f32)[:, None] * freq
    cos, sin = jnp.cos(angle), jnp.sin(angle)
    packed = project(
        hidden_in, gain_in, w_query, b_query, w_key, b_key, w_value, b_value, cos, sin
    )
    other = shifted(packed, "c", 1)
    first = jnp.where(even, packed, other)
    second = jnp.where(even, other, packed)
    q_width = w_query.shape[1]
    k_width = w_key.shape[1]
    queries = jnp.concatenate([first[:, :q_width], second[:, :q_width]], axis=1).reshape(
        slots, -1, head_size
    )
    key_raw = jnp.concatenate(
        [first[:, q_width : q_width + k_width], second[:, q_width : q_width + k_width]], axis=1
    )
    value_new = jnp.concatenate(
        [first[:, q_width + k_width :], second[:, q_width + k_width :]], axis=1
    )
    key_new = rotate(key_raw.astype(f32), cos, sin).astype(bf16)

    keys = k_cache[:, 0]
    values = v_cache[:, 0]
    scale = 1.0 / head_size**0.5
    scores = jnp.einsum("sgd,spd->sgp", queries, keys, preferred_element_type=f32) * scale
    place = c_pos * half_len + jnp.arange(half_len, dtype=jnp.int32)
    live = (place[None, :] < lens[:, None])[:, None, :]
    scores = jnp.where(live, scores, -1e30)
    own_score = (
        jnp.sum(queries.astype(f32) * key_new.astype(f32)[:, None, :], axis=2) * scale
    )
    own_score = jnp.where(even, own_score, -1e30)
    peak = jnp.maximum(jnp.max(scores, axis=2), own_score)
    weights = jnp.where(live, jnp.exp(scores - peak[..., None]), 0.0)
    own_weight = jnp.where(even, jnp.exp(own_score - peak), 0.0)
    total = jnp.sum(weights, axis=2) + own_weight
    mixed = jnp.einsum("sgp,spd->sgd", weights.astype(bf16), values, preferred_element_type=f32)
    mixed = mixed + own_weight[..., None] * value_new.astype(f32)[:, None, :]
    state_all = jnp.concatenate(
        [
            mixed,
            jnp.broadcast_to(peak[..., None], peak.shape + (head_size,)),
            jnp.broadcast_to(total[..., None], total.shape + (head_size,)),
        ],
        axis=2,
    )
    keep = jnp.where(even, state_all[:, :2], state_all[:, 2:])
    give = jnp.where(even, state_all[:, 2:], state_all[:, :2])
    got = shifted(give, "c", 1)
    peak_keep = keep[..., head_size : head_size + 1]
    peak_got = got[..., head_size : head_size + 1]
    upper = jnp.maximum(peak_keep, peak_got)
    mine = jnp.exp(peak_keep - upper)
    theirs = jnp.exp(peak_got - upper)
    merged = (keep[..., :head_size] * mine + got[..., :head_size] * theirs) / (
        keep[..., 2 * head_size : 2 * head_size + 1] * mine
        + got[..., 2 * head_size : 2 * head_size + 1] * theirs
    )
    attn = merged.reshape(slots, -1).astype(bf16)

    hits = own_bucket[None, :] == jnp.arange(serve, dtype=jnp.int32)[:, None]
    pick = jnp.max(jnp.where(hits, jnp.arange(slots, dtype=jnp.int32)[None, :], -1), axis=1)
    send_kv = pack(
        pick, lens - c_pos * half_len, k_cache, v_cache, key_new.astype(f32), value_new.astype(f32)
    )

    partial = jnp.dot(attn, w_out, preferred_element_type=f32).astype(bf16)
    partial = partial.reshape(2, rows, n_y, cols).transpose(2, 0, 1, 3).reshape(n_tp, rows, cols)
    shares = lax.all_to_all(partial, TP, split_axis=0, concat_axis=0, tiled=True)
    own_x = lax.dynamic_slice(hidden_in, (c_pos * rows, y_pos * cols), (rows, cols))
    state = (own_x.astype(f32) + jnp.sum(shares.astype(f32), axis=0)).astype(bf16)

    n_x = lax.axis_size("x")
    part = rows // 2
    by_z = spread(state, "z")
    part_a = by_z[:, :part].reshape(n_z * part, cols)
    part_b = by_z[:, part:].reshape(n_z * part, cols)
    from_x = [part_a] + [shifted(part_a, "x", d) for d in range(1, n_x)]
    from_y = [part_b] + [shifted(part_b, "y", d) for d in range(1, n_y)]
    by_z = after(by_z, send_kv)
    block_a = jnp.stack(from_x)
    block_b = jnp.stack(from_y)
    chunks_a = ring(block_a, "y")
    chunks_b = ring(block_b, "x")
    own_rows = lax.dynamic_slice(bucket, (0, c_pos * rows), (n_rep, rows))
    source = jnp.arange(n_rep, dtype=jnp.int32)[:, None]
    per_tp = n_rep // n_tp
    row = own_rows // cap * n_tp + source // per_tp
    lane = source % per_tp * cap + own_rows % cap

    def in_chunk_order(table):
        table = table.reshape(n_x, n_z, 2, part).transpose(2, 0, 1, 3)
        table = jnp.roll(table, -lax.axis_index("x"), axis=1)
        mirrored = jnp.concatenate([table[:, :1], table[:, :0:-1]], axis=1)
        return jnp.stack([table[0], jnp.where(even, table[1], mirrored[1])])

    steps = jnp.arange(n_y, dtype=jnp.int32)
    y_of_chunk = jnp.stack(
        [(y_pos + steps) % n_y, (y_pos + jnp.where(even, steps, n_y - steps)) % n_y]
    )

    row = in_chunk_order(row).reshape(1, -1)
    lane = in_chunk_order(lane).reshape(-1, 1)
    send = head(
        y_of_chunk, chunks_a, chunks_b, gain_out, row, lane, w_head, head_other, n_rep * n_tp
    )
    got = lax.all_to_all(send_kv, REP, split_axis=0, concat_axis=0, tiled=True)
    keys_out, values_out = settle(got)
    send = after(send, got)[:, None]
    arrived = lax.all_to_all(send, ALL, split_axis=0, concat_axis=0, tiled=True)
    arrived = after(arrived, keys_out)[:, 0]
    slots_here = per_tp * cap
    present = arrived[:, 2 * slots_here : 3 * slots_here] > 0.0
    best = jnp.max(jnp.where(present, arrived[:, :slots_here], -jnp.inf), axis=0)
    ms = jnp.max(arrived[:, slots_here : 2 * slots_here], axis=0)
    taken = jnp.any(present, axis=0)
    final_norm = jnp.where(taken, jnp.sqrt(ms), 0.0)
    top_logit = jnp.where(taken, best * lax.rsqrt(ms + eps), 0.0)
    return (final_norm, top_logit, keys_out, values_out)


def solution(mesh):
    n_rep, n_tp = mesh.devices.shape
    fine = Mesh(mesh.devices.reshape(4, n_rep // 4, n_tp // 2, 2), ("x", "z", "y", "c"))
    in_specs = (
        P(REP, None),
        P(REP, TP, None, None),
        P(REP, TP, None, None),
        P(),
        P(),
        P(None, TP),
        P(TP),
        P(None, TP),
        P(TP),
        P(None, TP),
        P(TP),
        P(TP, None),
        P(),
        P(),
        P(ALL, None),
    )
    out_specs = (P(ALL), P(ALL), P(REP, TP, None, None), P(REP, TP, None, None))
    return jax.shard_map(
        per_device, mesh=fine, in_specs=in_specs, out_specs=out_specs, check_vma=False
    )
```

```python
import jax
import jax.numpy as jnp
from jax import lax
from jax.experimental import pallas as pl
from jax.experimental.pallas import tpu as pltpu
from jax.sharding import Mesh, PartitionSpec as P

REP = ("x", "z")
TP = ("y", "c")
ALL = ("x", "z", "y", "c")
HBM = pltpu.MemorySpace.HBM
PER = 8


def shifted(value, axis, distance):
    size = lax.axis_size(axis)
    return lax.ppermute(value, axis, [((i + distance) % size, i) for i in range(size)])


def spread(value, axis):
    size = lax.axis_size(axis)
    copies = jnp.broadcast_to(value[None], (size,) + value.shape)
    return lax.all_to_all(copies, axis, split_axis=0, concat_axis=0, tiled=True)


def rotate(vals, cos, sin):
    half = vals.shape[-1] // 2
    first = vals[..., :half]
    second = vals[..., half:]
    return jnp.concatenate([first * cos - second * sin, second * cos + first * sin], axis=-1)


def ring(block, axis):
    size = lax.axis_size(axis)

    def from_side(value, step):
        pairs = [
            (((i + (step if c == 0 else -step)) % size) * 2 + c, i * 2 + c)
            for i in range(size)
            for c in range(2)
        ]
        return lax.ppermute(value, (axis, "c"), pairs)

    first = from_side(block, 1)
    second = from_side(block, -1)
    return [block, first, from_side(first, 1), second]


def head_kernel(y_ref, *refs):
    sources = refs[:8]
    gain, row, lane, own, other, out, x, weights = refs[8:16]
    landed = refs[16:24]
    chunk_sems, weight_sems = refs[24:]
    f32 = jnp.float32
    bf16 = jnp.bfloat16
    copies = [
        pltpu.make_async_copy(source, target, chunk_sems.at[i])
        for i, (source, target) in enumerate(zip(sources, landed))
    ]
    vocab, width = own.shape
    split = vocab // 16 * 8
    tiles = [(i, low, high) for i in range(2) for low, high in ((0, split), (split, vocab))]
    loads = [
        pltpu.make_async_copy(
            (own, other)[i].at[low:high], weights.at[i, low:high], weight_sems.at[at]
        )
        for at, (i, low, high) in enumerate(tiles)
    ]
    for copy in copies:
        copy.start()
    n, quarter, cols = landed[0].shape
    sums = [0.0] * (2 * n)
    def put(i, piece, chunk):
        start = pl.multiple_of(chunk * cols, 128)
        scale = gain[:, pl.ds(start, cols)].astype(f32)
        wide = piece.astype(f32)
        sums[i] = sums[i] + jnp.sum(wide * wide, axis=1, keepdims=True)
        x[pl.ds(i * quarter, quarter), pl.ds(start, cols)] = (wide * scale).astype(bf16)

    for d in range(n):
        copies[d].wait()
        for i in range(n):
            put(i, landed[d][i], y_ref[1, d])
    loads[0].start()
    for i in range(n):
        copies[n + i].wait()
        for d in range(n):
            put(n + i, landed[n + i][d], y_ref[0, d])
        if i == 0:
            for load in loads[1:]:
                load.start()
    dims = (((1,), (1,)), ((), ()))
    top = None
    for load, (i, low, high) in zip(loads, tiles):
        load.wait()
        logits = lax.dot_general(weights[i, low:high, :], x[...], dims, preferred_element_type=f32)
        peak = jnp.max(logits, axis=0, keepdims=True)
        top = peak if top is None else jnp.maximum(top, peak)

    ms = jnp.concatenate(sums, axis=0) / width
    top = jnp.transpose(jnp.broadcast_to(top, (8, top.shape[1])))[:, :1]
    at = lane[...]
    lanes = lax.broadcasted_iota(jnp.int32, (ms.shape[0], out.shape[1]), 1) - at
    spots = (lanes == 6 * PER).astype(f32)
    for i, value in enumerate((top, ms)):
        for j in range(3):
            term = value.astype(bf16).astype(f32)
            spots = spots + jnp.where(lanes == (3 * i + j) * PER, term, 0.0)
            value = value - term
    here = lax.broadcasted_iota(jnp.int32, (out.shape[0], row.shape[1]), 0) == row[...]
    moved = jnp.dot(here.astype(bf16), spots.astype(bf16), preferred_element_type=f32)

    def turned(terms):
        return pltpu.roll(moved, moved.shape[1] - terms * PER, 1)

    values = moved + turned(1) + turned(2)
    is_top = lax.broadcasted_iota(jnp.int32, out.shape, 1) < PER
    absent = is_top & (turned(6) == 0.0)
    out[...] = jnp.where(absent, -jnp.inf, values)


def head(y_pos, chunks_a, chunks_b, gain, row, lane, own, other, targets):
    chunks = chunks_a + chunks_b
    vocab, width = own.shape
    count = row.shape[1]
    vmem = pl.BlockSpec(memory_space=pltpu.VMEM)
    hbm = pl.BlockSpec(memory_space=HBM)
    return pl.pallas_call(
        head_kernel,
        in_specs=[pl.BlockSpec(memory_space=pltpu.SMEM)]
        + [hbm] * len(chunks)
        + [vmem] * 3
        + [hbm] * 2,
        out_specs=vmem,
        scratch_shapes=[
            pltpu.VMEM((count, width), jnp.bfloat16),
            pltpu.VMEM((2, vocab, width), jnp.bfloat16),
        ]
        + [pltpu.VMEM(value.shape, value.dtype) for value in chunks]
        + [pltpu.SemaphoreType.DMA((len(chunks),)), pltpu.SemaphoreType.DMA((4,))],
        out_shape=jax.ShapeDtypeStruct((targets, 128), jnp.float32),
        compiler_params=pltpu.CompilerParams(vmem_limit_bytes=60 * 1024 * 1024),
        name="head",
    )(y_pos, *chunks, gain[None], row, lane, own, other)


def after_kernel(value, other, out):
    del other, out


def after(value, *others):
    hbm = pl.BlockSpec(memory_space=HBM)
    for other in others:
        value = pl.pallas_call(
            after_kernel,
            in_specs=[hbm, hbm],
            out_specs=hbm,
            out_shape=jax.ShapeDtypeStruct(value.shape, value.dtype),
            input_output_aliases={0: 0},
            name="after",
        )(value, other)
    return value


def project_kernel(x_ref, gain, bias, cos, sin, wq_ref, wk_ref, wv_ref, out, wq, wk, wv, sems):
    f32 = jnp.float32
    bf16 = jnp.bfloat16
    loads = [
        pltpu.make_async_copy(source, target, sems.at[i])
        for i, (source, target) in enumerate(((wq_ref, wq), (wk_ref, wk), (wv_ref, wv)))
    ]
    for load in loads:
        load.start()
    x = x_ref[...].astype(f32)
    mean = jnp.mean(x * x, axis=1, keepdims=True)
    scale = gain[...].astype(f32)
    scale = jnp.concatenate([scale[i : i + 1] for i in range(scale.shape[0])], axis=1)
    normed = (x * lax.rsqrt(mean + 1e-06) * scale).astype(bf16)
    terms = bias[...].astype(f32)
    terms = jnp.concatenate([terms[i : i + 1] for i in range(terms.shape[0])], axis=1)
    for load in loads:
        load.wait()
    query = jnp.dot(normed, wq[...], preferred_element_type=f32)
    dims = (((1,), (1,)), ((), ()))
    rest = [
        lax.dot_general(normed, weight[...], dims, preferred_element_type=f32)
        for weight in (wk, wv)
    ]
    c, s = cos[...], sin[...]
    half = c.shape[1]
    at = query.shape[1]
    query = query + terms[:, :at]
    for low in range(0, at, 2 * half):
        first = query[:, low : low + half]
        second = query[:, low + half : low + 2 * half]
        out[:, low : low + 2 * half] = jnp.concatenate(
            [first * c - second * s, second * c + first * s], axis=1
        ).astype(bf16)
    out[:, at:] = (jnp.concatenate(rest, axis=1) + terms[:, at:]).astype(bf16)


def project(x, gain, wq, bq, wk, bk, wv, bv, cos, sin):
    width = wq.shape[1] + wk.shape[1] + wv.shape[1]
    vmem = pl.BlockSpec(memory_space=pltpu.VMEM)
    hbm = pl.BlockSpec(memory_space=HBM)
    weights = (wq, wk.T, wv.T)
    return pl.pallas_call(
        project_kernel,
        in_specs=[vmem] * 5 + [hbm] * 3,
        out_specs=vmem,
        out_shape=jax.ShapeDtypeStruct((x.shape[0], width), jnp.bfloat16),
        scratch_shapes=[pltpu.VMEM(w.shape, w.dtype) for w in weights]
        + [pltpu.SemaphoreType.DMA((3,))],
        compiler_params=pltpu.CompilerParams(vmem_limit_bytes=60 * 1024 * 1024),
        name="project",
    )(x, gain.reshape(-1, 128), jnp.concatenate([bq, bk, bv]).reshape(-1, 128), cos, sin, *weights)


def pack_kernel(pick, at, keys, values, key_new, value_new, out):
    half = keys.shape[2]
    place = lax.broadcasted_iota(jnp.int32, (half, keys.shape[3]), 0)

    def body(slot, carry):
        source = pick[slot]
        from_row = jnp.maximum(source, 0)
        live = jnp.broadcast_to(source, place.shape) >= 0
        written = place == at[from_row]
        for i, (cache, new) in enumerate(((keys, key_new), (values, value_new))):
            old = cache[from_row, 0].astype(jnp.float32)
            full = jnp.where(written, new[pl.ds(from_row, 1), :], old)
            out[slot, i * half : (i + 1) * half, :] = jnp.where(live, full, 0.0).astype(out.dtype)
        return carry

    lax.fori_loop(0, out.shape[0], body, 0, unroll=4)


def pack(pick, at, keys, values, key_new, value_new):
    _, _, half, head_size = keys.shape
    smem = pl.BlockSpec(memory_space=pltpu.SMEM)
    vmem = pl.BlockSpec(memory_space=pltpu.VMEM)
    return pl.pallas_call(
        pack_kernel,
        in_specs=[smem] * 2 + [vmem] * 4,
        out_specs=vmem,
        out_shape=jax.ShapeDtypeStruct((pick.shape[0], 2 * half, head_size), keys.dtype),
        compiler_params=pltpu.CompilerParams(vmem_limit_bytes=60 * 1024 * 1024),
        name="pack",
    )(pick, at, keys, values, key_new, value_new)


def settle_kernel(got, keys, values):
    half = keys.shape[2]
    keys[:, 0] = got[:, :half]
    values[:, 0] = got[:, half:]


def settle(got):
    serve, length, head_size = got.shape
    step = serve // 8
    shape = jax.ShapeDtypeStruct((serve, 1, length // 2, head_size), got.dtype)
    return pl.pallas_call(
        settle_kernel,
        grid=(8,),
        in_specs=[pl.BlockSpec((step, length, head_size), lambda i: (i, 0, 0))],
        out_specs=[pl.BlockSpec((step, 1, length // 2, head_size), lambda i: (i, 0, 0, 0))] * 2,
        out_shape=[shape, shape],
        name="settle",
    )(got)


def per_device(
    hidden_in,
    k_cache,
    v_cache,
    lengths,
    routes,
    w_query,
    b_query,
    w_key,
    b_key,
    w_value,
    b_value,
    w_out,
    gain_in,
    gain_out,
    w_head,
):
    f32 = jnp.float32
    bf16 = jnp.bfloat16
    eps = 1e-06
    n_z = lax.axis_size("z")
    n_y = lax.axis_size("y")
    n_rep = lax.axis_size("x") * n_z
    n_tp = n_y * 2
    y_pos = lax.axis_index("y")
    c_pos = lax.axis_index("c")
    rep_pos = lax.axis_index("x") * n_z + lax.axis_index("z")
    even = c_pos == 0
    slots, width = hidden_in.shape
    half_len, head_size = k_cache.shape[2:]
    cap = 2
    serve = n_rep * cap
    cols = width // n_y
    rows = slots // 2

    head_other = shifted(w_head, "c", 1)

    flat = routes[:, 0].reshape(n_rep, slots)
    earlier = (flat[:, None, :] == flat[:, :, None]) & (
        jnp.arange(slots)[None, None, :] < jnp.arange(slots)[None, :, None]
    )
    rank = jnp.sum(earlier.astype(jnp.int32), axis=2)
    bucket = flat * cap + rank
    own_bucket = lax.dynamic_slice_in_dim(bucket, rep_pos, 1, 0)[0]
    lens = lax.dynamic_slice_in_dim(lengths, rep_pos * slots, slots, 0)

    half = head_size // 2
    freq = 1000000.0 ** (-(jnp.arange(half, dtype=f32) * 2.0 / head_size))
    angle = lens.astype(f32)[:, None] * freq
    cos, sin = jnp.cos(angle), jnp.sin(angle)
    packed = project(
        hidden_in, gain_in, w_query, b_query, w_key, b_key, w_value, b_value, cos, sin
    )
    other = shifted(packed, "c", 1)
    first = jnp.where(even, packed, other)
    second = jnp.where(even, other, packed)
    q_width = w_query.shape[1]
    k_width = w_key.shape[1]
    queries = jnp.concatenate([first[:, :q_width], second[:, :q_width]], axis=1).reshape(
        slots, -1, head_size
    )
    key_raw = jnp.concatenate(
        [first[:, q_width : q_width + k_width], second[:, q_width : q_width + k_width]], axis=1
    )
    value_new = jnp.concatenate(
        [first[:, q_width + k_width :], second[:, q_width + k_width :]], axis=1
    )
    key_new = rotate(key_raw.astype(f32), cos, sin).astype(bf16)

    keys = k_cache[:, 0]
    values = v_cache[:, 0]
    scale = 1.0 / head_size**0.5
    scores = jnp.einsum("sgd,spd->sgp", queries, keys, preferred_element_type=f32) * scale
    place = c_pos * half_len + jnp.arange(half_len, dtype=jnp.int32)
    live = (place[None, :] < lens[:, None])[:, None, :]
    scores = jnp.where(live, scores, -1e30)
    own_score = (
        jnp.sum(queries.astype(f32) * key_new.astype(f32)[:, None, :], axis=2) * scale
    )
    own_score = jnp.where(even, own_score, -1e30)
    peak = jnp.maximum(jnp.max(scores, axis=2), own_score)
    weights = jnp.where(live, jnp.exp(scores - peak[..., None]), 0.0)
    own_weight = jnp.where(even, jnp.exp(own_score - peak), 0.0)
    total = jnp.sum(weights, axis=2) + own_weight
    mixed = jnp.einsum("sgp,spd->sgd", weights.astype(bf16), values, preferred_element_type=f32)
    mixed = mixed + own_weight[..., None] * value_new.astype(f32)[:, None, :]
    state_all = jnp.concatenate(
        [
            mixed,
            jnp.broadcast_to(peak[..., None], peak.shape + (head_size,)),
            jnp.broadcast_to(total[..., None], total.shape + (head_size,)),
        ],
        axis=2,
    )
    keep = jnp.where(even, state_all[:, :2], state_all[:, 2:])
    give = jnp.where(even, state_all[:, 2:], state_all[:, :2])
    got = shifted(give, "c", 1)
    peak_keep = keep[..., head_size : head_size + 1]
    peak_got = got[..., head_size : head_size + 1]
    upper = jnp.maximum(peak_keep, peak_got)
    mine = jnp.exp(peak_keep - upper)
    theirs = jnp.exp(peak_got - upper)
    merged = (keep[..., :head_size] * mine + got[..., :head_size] * theirs) / (
        keep[..., 2 * head_size : 2 * head_size + 1] * mine
        + got[..., 2 * head_size : 2 * head_size + 1] * theirs
    )
    attn = merged.reshape(slots, -1).astype(bf16)

    hits = own_bucket[None, :] == jnp.arange(serve, dtype=jnp.int32)[:, None]
    pick = jnp.max(jnp.where(hits, jnp.arange(slots, dtype=jnp.int32)[None, :], -1), axis=1)
    send_kv = pack(
        pick, lens - c_pos * half_len, k_cache, v_cache, key_new.astype(f32), value_new.astype(f32)
    )

    partial = jnp.dot(attn, w_out, preferred_element_type=f32).astype(bf16)
    partial = partial.reshape(2, rows, n_y, cols).transpose(2, 0, 1, 3).reshape(n_tp, rows, cols)
    shares = lax.all_to_all(partial, TP, split_axis=0, concat_axis=0, tiled=True)
    own_x = lax.dynamic_slice(hidden_in, (c_pos * rows, y_pos * cols), (rows, cols))
    state = (own_x.astype(f32) + jnp.sum(shares.astype(f32), axis=0)).astype(bf16)

    n_x = lax.axis_size("x")
    part = rows // 2
    by_z = spread(state, "z")
    part_b = by_z[:, part:].reshape(n_z * part, cols)
    part_a = by_z[:, :part].reshape(n_z * part, cols)
    from_y = [part_b] + [shifted(part_b, "y", d) for d in range(1, n_y)]
    late_a = after(part_a, from_y[1])
    from_x = [part_a] + [shifted(late_a, "x", d) for d in range(1, n_x)]
    by_z = after(by_z, send_kv)
    block_b = jnp.stack(from_y)
    block_a = jnp.stack(from_x)
    chunks_b = ring(block_b, "x")
    chunks_a = ring(block_a, "y")
    own_rows = lax.dynamic_slice(bucket, (0, c_pos * rows), (n_rep, rows))
    source = jnp.arange(n_rep, dtype=jnp.int32)[:, None]
    per_tp = n_rep // n_tp
    row = own_rows // cap * n_tp + source // per_tp
    lane = source % per_tp * cap + own_rows % cap

    tp_pos = y_pos * 2 + c_pos
    feeding = lax.dynamic_slice(bucket, (tp_pos * per_tp, 0), (per_tp, slots))
    own_buckets = rep_pos * cap + jnp.arange(cap, dtype=jnp.int32)
    taken = jnp.any(feeding[:, None, :] == own_buckets[None, :, None], axis=2).reshape(-1)

    def in_chunk_order(table):
        table = table.reshape(n_x, n_z, 2, part).transpose(2, 0, 1, 3)
        table = jnp.roll(table, -lax.axis_index("x"), axis=1)
        mirrored = jnp.concatenate([table[:, :1], table[:, :0:-1]], axis=1)
        return jnp.stack([table[0], jnp.where(even, table[1], mirrored[1])])

    steps = jnp.arange(n_y, dtype=jnp.int32)
    y_of_chunk = jnp.stack(
        [(y_pos + steps) % n_y, (y_pos + jnp.where(even, steps, n_y - steps)) % n_y]
    )

    row = in_chunk_order(row).reshape(1, -1)
    lane = in_chunk_order(lane).reshape(-1, 1)
    send = head(
        y_of_chunk, chunks_a, chunks_b, gain_out, row, lane, w_head, head_other, n_rep * n_tp
    )
    got = lax.all_to_all(send_kv, REP, split_axis=0, concat_axis=0, tiled=True)
    keys_out, values_out = settle(got)
    send = after(send, got)[:, None]
    arrived = lax.all_to_all(send, ALL, split_axis=0, concat_axis=0, tiled=True)
    arrived = jnp.max(after(arrived, keys_out), axis=(0, 1))
    best = arrived[:PER]
    ms = arrived[3 * PER : 4 * PER]
    final_norm = jnp.where(taken, jnp.sqrt(ms), 0.0)
    top_logit = jnp.where(taken, best * lax.rsqrt(ms + eps), 0.0)
    return (final_norm, top_logit, keys_out, values_out)


def solution(mesh):
    n_rep, n_tp = mesh.devices.shape
    fine = Mesh(mesh.devices.reshape(4, n_rep // 4, n_tp // 2, 2), ("x", "z", "y", "c"))
    in_specs = (
        P(REP, None),
        P(REP, TP, None, None),
        P(REP, TP, None, None),
        P(),
        P(),
        P(None, TP),
        P(TP),
        P(None, TP),
        P(TP),
        P(None, TP),
        P(TP),
        P(TP, None),
        P(),
        P(),
        P(ALL, None),
    )
    out_specs = (P(ALL), P(ALL), P(REP, TP, None, None), P(REP, TP, None, None))
    return jax.shard_map(
        per_device, mesh=fine, in_specs=in_specs, out_specs=out_specs, check_vma=False
    )
```

```python
import jax
import jax.numpy as jnp
from jax import lax
from jax.experimental import pallas as pl
from jax.experimental.pallas import tpu as pltpu
from jax.sharding import Mesh, PartitionSpec as P

REP = ("x", "z")
TP = ("y", "c")
ALL = ("x", "z", "y", "c")
HBM = pltpu.MemorySpace.HBM
PER = 8


def shifted(value, axis, distance):
    size = lax.axis_size(axis)
    return lax.ppermute(value, axis, [((i + distance) % size, i) for i in range(size)])


def spread(value, axis):
    size = lax.axis_size(axis)
    copies = jnp.broadcast_to(value[None], (size,) + value.shape)
    return lax.all_to_all(copies, axis, split_axis=0, concat_axis=0, tiled=True)


def rotate(vals, cos, sin):
    half = vals.shape[-1] // 2
    first = vals[..., :half]
    second = vals[..., half:]
    return jnp.concatenate([first * cos - second * sin, second * cos + first * sin], axis=-1)


def ring(block, axis):
    size = lax.axis_size(axis)

    def from_side(value, step):
        pairs = [
            (((i + (step if c == 0 else -step)) % size) * 2 + c, i * 2 + c)
            for i in range(size)
            for c in range(2)
        ]
        return lax.ppermute(value, (axis, "c"), pairs)

    first = from_side(block, 1)
    second = from_side(block, -1)
    return [block, first, from_side(first, 1), second]


def head_kernel(y_ref, *refs):
    sources = refs[:8]
    gain, row, lane, own, other, out, x, weights = refs[8:16]
    landed = refs[16:24]
    chunk_sems, weight_sems = refs[24:]
    f32 = jnp.float32
    bf16 = jnp.bfloat16
    copies = [
        pltpu.make_async_copy(source, target, chunk_sems.at[i])
        for i, (source, target) in enumerate(zip(sources, landed))
    ]
    vocab, width = own.shape
    split = vocab // 16 * 8
    tiles = [(i, low, high) for i in range(2) for low, high in ((0, split), (split, vocab))]
    loads = [
        pltpu.make_async_copy(
            (own, other)[i].at[low:high], weights.at[i, low:high], weight_sems.at[at]
        )
        for at, (i, low, high) in enumerate(tiles)
    ]
    for copy in copies:
        copy.start()
    n, quarter, cols = landed[0].shape
    sums = [0.0] * (2 * n)
    def put(i, piece, chunk):
        start = pl.multiple_of(chunk * cols, 128)
        scale = gain[:, pl.ds(start, cols)].astype(f32)
        wide = piece.astype(f32)
        sums[i] = sums[i] + jnp.sum(wide * wide, axis=1, keepdims=True)
        x[pl.ds(i * quarter, quarter), pl.ds(start, cols)] = (wide * scale).astype(bf16)

    for d in range(n):
        copies[d].wait()
        for i in range(n):
            put(i, landed[d][i], y_ref[1, d])
    loads[0].start()
    for i in range(n):
        copies[n + i].wait()
        for d in range(n):
            put(n + i, landed[n + i][d], y_ref[0, d])
        if i == 0:
            for load in loads[1:]:
                load.start()
    dims = (((1,), (1,)), ((), ()))
    top = None
    for load, (i, low, high) in zip(loads, tiles):
        load.wait()
        logits = lax.dot_general(weights[i, low:high, :], x[...], dims, preferred_element_type=f32)
        peak = jnp.max(logits, axis=0, keepdims=True)
        top = peak if top is None else jnp.maximum(top, peak)

    ms = jnp.concatenate(sums, axis=0) / width
    top = jnp.transpose(jnp.broadcast_to(top, (8, top.shape[1])))[:, :1]
    at = lane[...]
    lanes = lax.broadcasted_iota(jnp.int32, (ms.shape[0], out.shape[1]), 1) - at
    spots = (lanes == 6 * PER).astype(f32)
    for i, value in enumerate((top, ms)):
        for j in range(3):
            term = value.astype(bf16).astype(f32)
            spots = spots + jnp.where(lanes == (3 * i + j) * PER, term, 0.0)
            value = value - term
    here = lax.broadcasted_iota(jnp.int32, (out.shape[0], row.shape[1]), 0) == row[...]
    moved = jnp.dot(here.astype(bf16), spots.astype(bf16), preferred_element_type=f32)

    def turned(terms):
        return pltpu.roll(moved, moved.shape[1] - terms * PER, 1)

    values = moved + turned(1) + turned(2)
    is_top = lax.broadcasted_iota(jnp.int32, out.shape, 1) < PER
    absent = is_top & (turned(6) == 0.0)
    out[...] = jnp.where(absent, -jnp.inf, values)


def head(y_pos, chunks_a, chunks_b, gain, row, lane, own, other, targets):
    chunks = chunks_a + chunks_b
    vocab, width = own.shape
    count = row.shape[1]
    vmem = pl.BlockSpec(memory_space=pltpu.VMEM)
    hbm = pl.BlockSpec(memory_space=HBM)
    return pl.pallas_call(
        head_kernel,
        in_specs=[pl.BlockSpec(memory_space=pltpu.SMEM)]
        + [hbm] * len(chunks)
        + [vmem] * 3
        + [hbm] * 2,
        out_specs=vmem,
        scratch_shapes=[
            pltpu.VMEM((count, width), jnp.bfloat16),
            pltpu.VMEM((2, vocab, width), jnp.bfloat16),
        ]
        + [pltpu.VMEM(value.shape, value.dtype) for value in chunks]
        + [pltpu.SemaphoreType.DMA((len(chunks),)), pltpu.SemaphoreType.DMA((4,))],
        out_shape=jax.ShapeDtypeStruct((targets, 128), jnp.float32),
        compiler_params=pltpu.CompilerParams(vmem_limit_bytes=60 * 1024 * 1024),
        name="head",
    )(y_pos, *chunks, gain[None], row, lane, own, other)


def after_kernel(value, other, out):
    del other, out


def after(value, *others):
    hbm = pl.BlockSpec(memory_space=HBM)
    for other in others:
        value = pl.pallas_call(
            after_kernel,
            in_specs=[hbm, hbm],
            out_specs=hbm,
            out_shape=jax.ShapeDtypeStruct(value.shape, value.dtype),
            input_output_aliases={0: 0},
            name="after",
        )(value, other)
    return value


def project_kernel(x_ref, gain, bias, cos, sin, wq_ref, wk_ref, wv_ref, out, wq, wk, wv, sems):
    f32 = jnp.float32
    bf16 = jnp.bfloat16
    loads = [
        pltpu.make_async_copy(source, target, sems.at[i])
        for i, (source, target) in enumerate(((wq_ref, wq), (wk_ref, wk), (wv_ref, wv)))
    ]
    for load in loads:
        load.start()
    x = x_ref[...].astype(f32)
    mean = jnp.mean(x * x, axis=1, keepdims=True)
    scale = gain[...].astype(f32)
    scale = jnp.concatenate([scale[i : i + 1] for i in range(scale.shape[0])], axis=1)
    normed = (x * lax.rsqrt(mean + 1e-06) * scale).astype(bf16)
    terms = bias[...].astype(f32)
    terms = jnp.concatenate([terms[i : i + 1] for i in range(terms.shape[0])], axis=1)
    for load in loads:
        load.wait()
    query = jnp.dot(normed, wq[...], preferred_element_type=f32)
    dims = (((1,), (1,)), ((), ()))
    rest = [
        lax.dot_general(normed, weight[...], dims, preferred_element_type=f32)
        for weight in (wk, wv)
    ]
    c, s = cos[...], sin[...]
    half = c.shape[1]
    at = query.shape[1]
    query = query + terms[:, :at]
    for low in range(0, at, 2 * half):
        first = query[:, low : low + half]
        second = query[:, low + half : low + 2 * half]
        out[:, low : low + 2 * half] = jnp.concatenate(
            [first * c - second * s, second * c + first * s], axis=1
        ).astype(bf16)
    out[:, at:] = (jnp.concatenate(rest, axis=1) + terms[:, at:]).astype(bf16)


def project(x, gain, wq, bq, wk, bk, wv, bv, cos, sin):
    width = wq.shape[1] + wk.shape[1] + wv.shape[1]
    vmem = pl.BlockSpec(memory_space=pltpu.VMEM)
    hbm = pl.BlockSpec(memory_space=HBM)
    weights = (wq, wk.T, wv.T)
    return pl.pallas_call(
        project_kernel,
        in_specs=[vmem] * 5 + [hbm] * 3,
        out_specs=vmem,
        out_shape=jax.ShapeDtypeStruct((x.shape[0], width), jnp.bfloat16),
        scratch_shapes=[pltpu.VMEM(w.shape, w.dtype) for w in weights]
        + [pltpu.SemaphoreType.DMA((3,))],
        compiler_params=pltpu.CompilerParams(vmem_limit_bytes=60 * 1024 * 1024),
        name="project",
    )(x, gain.reshape(-1, 128), jnp.concatenate([bq, bk, bv]).reshape(-1, 128), cos, sin, *weights)


def pack_kernel(pick, at, keys, values, key_new, value_new, out):
    half = keys.shape[2]
    place = lax.broadcasted_iota(jnp.int32, (half, keys.shape[3]), 0)

    def body(slot, carry):
        source = pick[slot]
        from_row = jnp.maximum(source, 0)
        live = jnp.broadcast_to(source, place.shape) >= 0
        written = place == at[from_row]
        for i, (cache, new) in enumerate(((keys, key_new), (values, value_new))):
            old = cache[from_row, 0].astype(jnp.float32)
            full = jnp.where(written, new[pl.ds(from_row, 1), :], old)
            out[slot, i * half : (i + 1) * half, :] = jnp.where(live, full, 0.0).astype(out.dtype)
        return carry

    lax.fori_loop(0, out.shape[0], body, 0, unroll=4)


def pack(pick, at, keys, values, key_new, value_new):
    _, _, half, head_size = keys.shape
    smem = pl.BlockSpec(memory_space=pltpu.SMEM)
    vmem = pl.BlockSpec(memory_space=pltpu.VMEM)
    return pl.pallas_call(
        pack_kernel,
        in_specs=[smem] * 2 + [vmem] * 4,
        out_specs=vmem,
        out_shape=jax.ShapeDtypeStruct((pick.shape[0], 2 * half, head_size), keys.dtype),
        compiler_params=pltpu.CompilerParams(vmem_limit_bytes=60 * 1024 * 1024),
        name="pack",
    )(pick, at, keys, values, key_new, value_new)


def settle_kernel(got, keys, values):
    half = keys.shape[2]
    keys[:, 0] = got[:, :half]
    values[:, 0] = got[:, half:]


def settle(got):
    serve, length, head_size = got.shape
    step = serve // 8
    shape = jax.ShapeDtypeStruct((serve, 1, length // 2, head_size), got.dtype)
    return pl.pallas_call(
        settle_kernel,
        grid=(8,),
        in_specs=[pl.BlockSpec((step, length, head_size), lambda i: (i, 0, 0))],
        out_specs=[pl.BlockSpec((step, 1, length // 2, head_size), lambda i: (i, 0, 0, 0))] * 2,
        out_shape=[shape, shape],
        name="settle",
    )(got)


def per_device(
    hidden_in,
    k_cache,
    v_cache,
    lengths,
    routes,
    w_query,
    b_query,
    w_key,
    b_key,
    w_value,
    b_value,
    w_out,
    gain_in,
    gain_out,
    w_head,
):
    f32 = jnp.float32
    bf16 = jnp.bfloat16
    eps = 1e-06
    n_z = lax.axis_size("z")
    n_y = lax.axis_size("y")
    n_rep = lax.axis_size("x") * n_z
    n_tp = n_y * 2
    y_pos = lax.axis_index("y")
    c_pos = lax.axis_index("c")
    rep_pos = lax.axis_index("x") * n_z + lax.axis_index("z")
    even = c_pos == 0
    slots, width = hidden_in.shape
    half_len, head_size = k_cache.shape[2:]
    cap = 2
    serve = n_rep * cap
    cols = width // n_y
    rows = slots // 2

    head_other = shifted(w_head, "c", 1)

    flat = routes[:, 0].reshape(n_rep, slots)
    earlier = (flat[:, None, :] == flat[:, :, None]) & (
        jnp.arange(slots)[None, None, :] < jnp.arange(slots)[None, :, None]
    )
    rank = jnp.sum(earlier.astype(jnp.int32), axis=2)
    bucket = flat * cap + rank
    own_bucket = lax.dynamic_slice_in_dim(bucket, rep_pos, 1, 0)[0]
    lens = lax.dynamic_slice_in_dim(lengths, rep_pos * slots, slots, 0)

    half = head_size // 2
    freq = 1000000.0 ** (-(jnp.arange(half, dtype=f32) * 2.0 / head_size))
    angle = lens.astype(f32)[:, None] * freq
    cos, sin = jnp.cos(angle), jnp.sin(angle)
    packed = project(
        hidden_in, gain_in, w_query, b_query, w_key, b_key, w_value, b_value, cos, sin
    )
    other = shifted(packed, "c", 1)
    first = jnp.where(even, packed, other)
    second = jnp.where(even, other, packed)
    q_width = w_query.shape[1]
    k_width = w_key.shape[1]
    queries = jnp.concatenate([first[:, :q_width], second[:, :q_width]], axis=1).reshape(
        slots, -1, head_size
    )
    key_raw = jnp.concatenate(
        [first[:, q_width : q_width + k_width], second[:, q_width : q_width + k_width]], axis=1
    )
    value_new = jnp.concatenate(
        [first[:, q_width + k_width :], second[:, q_width + k_width :]], axis=1
    )
    key_new = rotate(key_raw.astype(f32), cos, sin).astype(bf16)

    keys = k_cache[:, 0]
    values = v_cache[:, 0]
    scale = 1.0 / head_size**0.5
    scores = jnp.einsum("sgd,spd->sgp", queries, keys, preferred_element_type=f32) * scale
    place = c_pos * half_len + jnp.arange(half_len, dtype=jnp.int32)
    live = (place[None, :] < lens[:, None])[:, None, :]
    scores = jnp.where(live, scores, -1e30)
    own_score = (
        jnp.sum(queries.astype(f32) * key_new.astype(f32)[:, None, :], axis=2) * scale
    )
    own_score = jnp.where(even, own_score, -1e30)
    peak = jnp.maximum(jnp.max(scores, axis=2), own_score)
    weights = jnp.where(live, jnp.exp(scores - peak[..., None]), 0.0)
    own_weight = jnp.where(even, jnp.exp(own_score - peak), 0.0)
    total = jnp.sum(weights, axis=2) + own_weight
    mixed = jnp.einsum("sgp,spd->sgd", weights.astype(bf16), values, preferred_element_type=f32)
    mixed = mixed + own_weight[..., None] * value_new.astype(f32)[:, None, :]
    state_all = jnp.concatenate(
        [
            mixed,
            jnp.broadcast_to(peak[..., None], peak.shape + (head_size,)),
            jnp.broadcast_to(total[..., None], total.shape + (head_size,)),
        ],
        axis=2,
    )
    keep = jnp.where(even, state_all[:, :2], state_all[:, 2:])
    give = jnp.where(even, state_all[:, 2:], state_all[:, :2])
    got = shifted(give, "c", 1)
    peak_keep = keep[..., head_size : head_size + 1]
    peak_got = got[..., head_size : head_size + 1]
    upper = jnp.maximum(peak_keep, peak_got)
    mine = jnp.exp(peak_keep - upper)
    theirs = jnp.exp(peak_got - upper)
    merged = (keep[..., :head_size] * mine + got[..., :head_size] * theirs) / (
        keep[..., 2 * head_size : 2 * head_size + 1] * mine
        + got[..., 2 * head_size : 2 * head_size + 1] * theirs
    )
    attn = merged.reshape(slots, -1).astype(bf16)

    hits = own_bucket[None, :] == jnp.arange(serve, dtype=jnp.int32)[:, None]
    pick = jnp.max(jnp.where(hits, jnp.arange(slots, dtype=jnp.int32)[None, :], -1), axis=1)
    send_kv = pack(
        pick, lens - c_pos * half_len, k_cache, v_cache, key_new.astype(f32), value_new.astype(f32)
    )

    partial = jnp.dot(attn, w_out, preferred_element_type=f32).astype(bf16)
    partial = partial.reshape(2, rows, n_y, cols).transpose(2, 0, 1, 3).reshape(n_tp, rows, cols)
    shares = lax.all_to_all(partial, TP, split_axis=0, concat_axis=0, tiled=True)
    own_x = lax.dynamic_slice(hidden_in, (c_pos * rows, y_pos * cols), (rows, cols))
    state = (own_x.astype(f32) + jnp.sum(shares.astype(f32), axis=0)).astype(bf16)

    n_x = lax.axis_size("x")
    part = rows // 2
    by_z = spread(state, "z")
    part_b = by_z[:, part:].reshape(n_z * part, cols)
    part_a = by_z[:, :part].reshape(n_z * part, cols)
    from_y = [part_b] + [shifted(part_b, "y", d) for d in range(1, n_y)]
    late_a = after(part_a, from_y[1])
    send_kv = after(send_kv, from_y[1])
    from_x = [part_a] + [shifted(late_a, "x", d) for d in range(1, n_x)]
    by_z = after(by_z, send_kv)
    block_b = jnp.stack(from_y)
    block_a = jnp.stack(from_x)
    chunks_b = ring(block_b, "x")
    chunks_a = ring(block_a, "y")
    own_rows = lax.dynamic_slice(bucket, (0, c_pos * rows), (n_rep, rows))
    source = jnp.arange(n_rep, dtype=jnp.int32)[:, None]
    per_tp = n_rep // n_tp
    row = own_rows // cap * n_tp + source // per_tp
    lane = source % per_tp * cap + own_rows % cap

    tp_pos = y_pos * 2 + c_pos
    feeding = lax.dynamic_slice(bucket, (tp_pos * per_tp, 0), (per_tp, slots))
    own_buckets = rep_pos * cap + jnp.arange(cap, dtype=jnp.int32)
    taken = jnp.any(feeding[:, None, :] == own_buckets[None, :, None], axis=2).reshape(-1)

    def in_chunk_order(table):
        table = table.reshape(n_x, n_z, 2, part).transpose(2, 0, 1, 3)
        table = jnp.roll(table, -lax.axis_index("x"), axis=1)
        mirrored = jnp.concatenate([table[:, :1], table[:, :0:-1]], axis=1)
        return jnp.stack([table[0], jnp.where(even, table[1], mirrored[1])])

    steps = jnp.arange(n_y, dtype=jnp.int32)
    y_of_chunk = jnp.stack(
        [(y_pos + steps) % n_y, (y_pos + jnp.where(even, steps, n_y - steps)) % n_y]
    )

    row = in_chunk_order(row).reshape(1, -1)
    lane = in_chunk_order(lane).reshape(-1, 1)
    send = head(
        y_of_chunk, chunks_a, chunks_b, gain_out, row, lane, w_head, head_other, n_rep * n_tp
    )
    got = lax.all_to_all(send_kv, REP, split_axis=0, concat_axis=0, tiled=True)
    keys_out, values_out = settle(got)
    send = after(send, got)[:, None]
    arrived = lax.all_to_all(send, ALL, split_axis=0, concat_axis=0, tiled=True)
    arrived = jnp.max(after(arrived, keys_out), axis=(0, 1))
    best = arrived[:PER]
    ms = arrived[3 * PER : 4 * PER]
    final_norm = jnp.where(taken, jnp.sqrt(ms), 0.0)
    top_logit = jnp.where(taken, best * lax.rsqrt(ms + eps), 0.0)
    return (final_norm, top_logit, keys_out, values_out)


def solution(mesh):
    n_rep, n_tp = mesh.devices.shape
    fine = Mesh(mesh.devices.reshape(4, n_rep // 4, n_tp // 2, 2), ("x", "z", "y", "c"))
    in_specs = (
        P(REP, None),
        P(REP, TP, None, None),
        P(REP, TP, None, None),
        P(),
        P(),
        P(None, TP),
        P(TP),
        P(None, TP),
        P(TP),
        P(None, TP),
        P(TP),
        P(TP, None),
        P(),
        P(),
        P(ALL, None),
    )
    out_specs = (P(ALL), P(ALL), P(REP, TP, None, None), P(REP, TP, None, None))
    return jax.shard_map(
        per_device, mesh=fine, in_specs=in_specs, out_specs=out_specs, check_vma=False
    )
```
